256 devices in a mesh: seq: 128 (over y, z, x), head: 2 (over core).
Axes of the slice: x: 4, y: 4, z: 8, core: 2. Of those that a mesh axis runs over, the one named last changes fastest.
Arguments:
- queries: bfloat16 [32768, 4096], P('seq', 'head'), may hold values from -6 to 6
- keys: bfloat16 [32768, 4096], P('seq', 'head'), may hold values from -6 to 6
- values: bfloat16 [32768, 4096], P('seq', 'head'), may hold values from -6 to 6
- gain: float32 [4096], P('head'), may hold values from 0.1 to 1.9
- w_out: bfloat16 [4096, 3072], P('head', 'seq'), may hold values from -0.09375 to 0.09375
Outputs:
- mixed: bfloat16 [32768, 3072], P(('seq', 'head'))
The draws below stay inside these ranges and needn't reach their ends.
All inputs are finite; a program needn't handle non-finite values.
Results may differ from the reference program's by a relative error of at most 0.0049.
Values may be sent and summed in bfloat16 or wider, within the bound.
No kernel may reach another device: no remote copies, remote signals or barrier semaphores. Data moves between devices by JAX's collectives and lax.ppermute only.
A program may use at most 320 MiB of HBM per device.

```python
import math
import jax
import jax.numpy as jnp
from jax import lax

D = 3072
HEADS = 32
DH = 128
TOKENS = 32768


def levels(stream_key, dims, cuts, smallest, largest):
    factor_of, own = 1.0, jax.random.fold_in(stream_key, 6)
    for dim, shards_of in cuts:
        steps = jnp.exp(jax.random.uniform(jax.random.fold_in(own, dim), (shards_of,), jnp.float32, smallest / len(cuts), largest / len(cuts)))
        factor_of = factor_of * jnp.repeat(steps, dims[dim] // shards_of).reshape([-1 if axis == dim else 1 for axis in range(len(dims))])
    return factor_of


def normal_values(key, extent, width, most, shards=(), kind=jnp.bfloat16):
    array = width * jax.random.normal(key, extent, jnp.float32)
    if shards:
        array = array * levels(key, extent, shards, -0.22, 0.18)
    return jnp.clip(array, -most, most).astype(kind)


def setup_inputs(seed: int = 0) -> dict:
    key_list = jax.random.split(jax.random.key(seed), 6)
    queries = normal_values(key_list[0], (TOKENS, HEADS * DH), 1.0, 6.0, ((0, 128), (1, 2)))
    keys = normal_values(key_list[1], (TOKENS, HEADS * DH), 1.0, 6.0, ((0, 128), (1, 2)))
    values = normal_values(key_list[2], (TOKENS, HEADS * DH), 1.0, 6.0, ((0, 128), (1, 2)))
    gain = jnp.clip(1.0 + 0.18 * jax.random.normal(key_list[3], (HEADS * DH,), jnp.float32), 0.1, 1.9)
    w_out = normal_values(key_list[4], (HEADS * DH, D), (HEADS * DH) ** -0.5, 0.09375, ((0, 2), (1, 128)))
    return {"queries": queries, "keys": keys, "values": values, "gain": gain, "w_out": w_out}


def reference(queries, keys, values, gain, w_out):
    length = queries.shape[0]
    block_rows = math.gcd(length, 512)
    blocks = length // block_rows
    query_all = queries.reshape(blocks, block_rows, HEADS, DH)
    key_all = keys.reshape(blocks, block_rows, HEADS, DH)
    value_all = values.reshape(blocks, block_rows, HEADS, DH)
    causal_mask = jnp.arange(block_rows)[:, None] >= jnp.arange(block_rows)[None, :]
    gain_rows = gain.reshape(HEADS, DH)
    highest = lax.Precision.HIGHEST

    def advance(carried, inputs):
        query_block, key_block, value_block = inputs
        query_f = query_block.astype(jnp.float32)
        key_f = key_block.astype(jnp.float32)
        value_f = value_block.astype(jnp.float32)
        cross = jnp.einsum('thd,hde->the', query_f, carried, precision=highest)
        scores = jnp.einsum('thd,shd->hts', query_f, key_f, precision=highest)
        scores = jnp.where(causal_mask[None], scores, jnp.float32(0.0))
        inner = jnp.einsum('hts,she->the', scores, value_f, precision=highest)
        attn = cross + inner
        carried = carried + jnp.einsum('thd,the->hde', key_f, value_f, precision=highest)
        meansq = lax.optimization_barrier(jnp.mean(attn * attn, axis=-1, keepdims=True))
        normed = (attn * lax.rsqrt(meansq + 1e-06) * gain_rows).astype(jnp.bfloat16)
        normed = normed.reshape(block_rows, HEADS * DH)
        result = jnp.dot(normed, w_out, preferred_element_type=jnp.float32).astype(jnp.bfloat16)
        return (carried, result)
    initial = jnp.zeros((HEADS, DH, DH), jnp.float32)
    _, results = lax.scan(advance, initial, (query_all, key_all, value_all))
    return results.reshape(length, D)
```

```python
import jax
import jax.numpy as jnp
from jax import lax
from jax.experimental import pallas as pl
from jax.experimental.pallas import tpu as pltpu
from jax.sharding import PartitionSpec as P

DH = 128
BF = jnp.bfloat16
F32 = jnp.float32


def dot(a, b, dims):
    return lax.dot_general(a, b, (dims, ((), ())), preferred_element_type=F32)


def states_kernel(k_ref, v_ref, o_ref):
    for h in range(k_ref.shape[1] // DH):
        c = slice(h * DH, (h + 1) * DH)
        o_ref[c, :] = dot(k_ref[:, c], v_ref[:, c], ((0,), (0,))).astype(BF)


def local_states(keys, values, heads_per_step=4):
    rows, cols = keys.shape
    width = heads_per_step * DH
    spec = pl.BlockSpec((rows, width), lambda i: (0, i))
    return pl.pallas_call(
        states_kernel,
        grid=(cols // width,),
        in_specs=[spec, spec],
        out_specs=pl.BlockSpec((width, DH), lambda i: (i, 0)),
        out_shape=jax.ShapeDtypeStruct((cols, DH), BF),
        name="local_states",
    )(keys, values)


def running_kernel(x_ref, o_ref):
    def step(j, total):
        o_ref[j] = total.astype(BF)
        return total + x_ref[j].astype(F32)

    lax.fori_loop(0, x_ref.shape[0], step, jnp.zeros(x_ref.shape[1:], F32), unroll=8)


def exclusive_sums(pieces):
    return pl.pallas_call(
        running_kernel,
        out_shape=jax.ShapeDtypeStruct(pieces.shape, BF),
        name="exclusive_sums",
    )(pieces)


def attention_kernel(q_ref, k_ref, v_ref, s_ref, g_ref, o_ref):
    rows = q_ref.shape[0]
    t = lax.broadcasted_iota(jnp.int32, (rows, rows), 0)
    s = lax.broadcasted_iota(jnp.int32, (rows, rows), 1)
    causal = t >= s
    for h in range(q_ref.shape[1] // DH):
        c = slice(h * DH, (h + 1) * DH)
        q, k, v = q_ref[:, c], k_ref[:, c], v_ref[:, c]
        scores = jnp.where(causal, dot(q, k, ((1,), (1,))), 0.0)
        high = scores.astype(BF)
        low = (scores - high.astype(F32)).astype(BF)
        attn = dot(q, s_ref[c, :], ((1,), (0,)))
        attn = attn + dot(high, v, ((1,), (0,)))
        attn = attn + dot(low, v, ((1,), (0,)))
        meansq = jnp.mean(attn * attn, axis=-1, keepdims=True)
        o_ref[:, c] = (attn * lax.rsqrt(meansq + 1e-06) * g_ref[:, c]).astype(BF)


def attention(queries, keys, values, prior, gain, heads_per_step=4):
    rows, cols = queries.shape
    width = heads_per_step * DH
    spec = pl.BlockSpec((rows, width), lambda i: (0, i))
    return pl.pallas_call(
        attention_kernel,
        grid=(cols // width,),
        in_specs=[
            spec,
            spec,
            spec,
            pl.BlockSpec((width, DH), lambda i: (i, 0)),
            pl.BlockSpec((1, width), lambda i: (0, i)),
        ],
        out_specs=spec,
        out_shape=jax.ShapeDtypeStruct((rows, cols), BF),
        name="attention",
    )(queries, keys, values, prior, gain)


def project_kernel(place_ref, n_ref, w_ref, mine_ref, theirs_ref):
    half = mine_ref.shape[0]
    me = place_ref[0]
    terms = dot(n_ref[...], w_ref[...], ((1,), (1,)))
    first, second = terms[:half], terms[half:]
    mine_ref[...] = jnp.where(me == 0, first, second)
    theirs_ref[...] = jnp.where(me == 0, second, first)


def project(place, normed, w_rows, block=384):
    rows, depth = normed.shape
    width = w_rows.shape[0]
    half = jax.ShapeDtypeStruct((rows // 2, width), F32)
    out = pl.BlockSpec((rows // 2, block), lambda i, p: (0, i))
    return pl.pallas_call(
        project_kernel,
        grid_spec=pltpu.PrefetchScalarGridSpec(
            num_scalar_prefetch=1,
            grid=(width // block,),
            in_specs=[
                pl.BlockSpec((rows, depth), lambda i, p: (0, 0)),
                pl.BlockSpec((block, depth), lambda i, p: (i, 0)),
            ],
            out_specs=[out, out],
        ),
        out_shape=[half, half],
        name="project",
    )(place, normed, w_rows)


def per_device(queries, keys, values, gain, w_out):
    devices = lax.axis_size("seq")
    w_rows = lax.all_gather(w_out.T, "seq", axis=0, tiled=True)
    states = local_states(keys, values)
    pieces = lax.all_to_all(states, "seq", 0, 0, tiled=True)
    sums = exclusive_sums(pieces.reshape(devices, -1, DH))
    prior = lax.all_to_all(sums.reshape(-1, DH), "seq", 0, 0, tiled=True)
    normed = attention(queries, keys, values, prior, gain.reshape(1, -1))
    place = lax.axis_index("head").astype(jnp.int32).reshape(1)
    mine, theirs = project(place, normed, w_rows)
    other = lax.ppermute(theirs, "head", [(0, 1), (1, 0)])
    return (mine + other).astype(BF)


def solution(mesh):
    return jax.shard_map(
        per_device,
        mesh=mesh,
        in_specs=(
            P("seq", "head"),
            P("seq", "head"),
            P("seq", "head"),
            P("head"),
            P("head", "seq"),
        ),
        out_specs=P(("seq", "head"), None),
        check_vma=False,
    )
```

```python
import jax
import jax.numpy as jnp
from jax import lax
from jax.experimental import pallas as pl
from jax.experimental.pallas import tpu as pltpu
from jax.sharding import PartitionSpec as P


DH = 128
BF = jnp.bfloat16
F32 = jnp.float32


def dot(a, b, dims):
    return lax.dot_general(a, b, (dims, ((), ())), preferred_element_type=F32)


def states_kernel(k_ref, v_ref, o_ref):
    for h in range(k_ref.shape[1] // DH):
        c = slice(h * DH, (h + 1) * DH)
        o_ref[c, :] = dot(k_ref[:, c], v_ref[:, c], ((0,), (0,))).astype(BF)


def local_states(keys, values, heads_per_step=4):
    rows, cols = keys.shape
    width = heads_per_step * DH
    spec = pl.BlockSpec((rows, width), lambda i: (0, i))
    return pl.pallas_call(
        states_kernel,
        grid=(cols // width,),
        in_specs=[spec, spec],
        out_specs=pl.BlockSpec((width, DH), lambda i: (i, 0)),
        out_shape=jax.ShapeDtypeStruct((cols, DH), BF),
        name="local_states",
    )(keys, values)


def running_kernel(x_ref, o_ref):
    def step(j, total):
        o_ref[j] = total.astype(BF)
        return total + x_ref[j].astype(F32)

    lax.fori_loop(0, x_ref.shape[0], step, jnp.zeros(x_ref.shape[1:], F32), unroll=8)


def exclusive_sums(pieces):
    return pl.pallas_call(
        running_kernel,
        out_shape=jax.ShapeDtypeStruct(pieces.shape, BF),
        name="exclusive_sums",
    )(pieces)


def attention_kernel(q_ref, k_ref, v_ref, s_ref, g_ref, o_ref):
    rows = q_ref.shape[0]
    t = lax.broadcasted_iota(jnp.int32, (rows, rows), 0)
    s = lax.broadcasted_iota(jnp.int32, (rows, rows), 1)
    causal = t >= s
    for h in range(q_ref.shape[1] // DH):
        c = slice(h * DH, (h + 1) * DH)
        q, k, v = q_ref[:, c], k_ref[:, c], v_ref[:, c]
        scores = jnp.where(causal, dot(q, k, ((1,), (1,))), 0.0)
        high = scores.astype(BF)
        low = (scores - high.astype(F32)).astype(BF)
        attn = dot(q, s_ref[c, :], ((1,), (0,)))
        attn = attn + dot(high, v, ((1,), (0,)))
        attn = attn + dot(low, v, ((1,), (0,)))
        meansq = jnp.mean(attn * attn, axis=-1, keepdims=True)
        o_ref[:, c] = (attn * lax.rsqrt(meansq + 1e-06) * g_ref[:, c]).astype(BF)


def attention(queries, keys, values, prior, gain, heads_per_step=4):
    rows, cols = queries.shape
    width = heads_per_step * DH
    spec = pl.BlockSpec((rows, width), lambda i: (0, i))
    return pl.pallas_call(
        attention_kernel,
        grid=(cols // width,),
        in_specs=[
            spec,
            spec,
            spec,
            pl.BlockSpec((width, DH), lambda i: (i, 0)),
            pl.BlockSpec((1, width), lambda i: (0, i)),
        ],
        out_specs=spec,
        out_shape=jax.ShapeDtypeStruct((rows, cols), BF),
        name="attention",
    )(queries, keys, values, prior, gain)


SEQ = ("y", "z", "x")
NY, NZ, NX = 4, 8, 4
PART_B, PART_C = 1024, 1024


def shift(block, axis, by):
    pairs = []
    for y in range(NY):
        for z in range(NZ):
            for x in range(NX):
                ty = (y + by) % NY if axis == "y" else y
                tz = (z + by) % NZ if axis == "z" else z
                tx = (x + by) % NX if axis == "x" else x
                pairs.append(((y * NZ + z) * NX + x, (ty * NZ + tz) * NX + tx))
    return lax.ppermute(block, SEQ, pairs)


def wrap(index, count):
    return lax.rem(index + count, count)


def assemble(place, which, pieces, outs, cuts):
    count = len(pieces)

    def kernel(place_ref, *refs):
        for by in range(count):
            cuts(refs[by], refs[count:], wrap(place_ref[which] - by, count))

    vmem = pl.BlockSpec(memory_space=pltpu.VMEM)
    return pl.pallas_call(
        kernel,
        in_specs=[pl.BlockSpec(memory_space=pltpu.SMEM)] + [vmem] * count,
        out_specs=[vmem] * len(outs),
        out_shape=[jax.ShapeDtypeStruct(o, BF) for o in outs],
    )(place, *pieces)


def both_ways(low, high, axis):
    below_low = shift(low, axis, 1)
    above_high = shift(high, axis, -1)
    below_high = shift(high, axis, 1)
    above_low = shift(low, axis, -1)
    far_low = shift(below_low, axis, 1)
    far_high = shift(above_high, axis, -1)
    return [low, high, below_low, below_high, far_low, far_high, above_low, above_high]


def gather(own, place):
    n = own.shape[0]
    half = NZ // 2
    pieces = [own] + [shift(own, "z", by) for by in range(1, NZ)]

    def cut_z(piece, outs, i):
        outs[0][i] = piece[:, :PART_B]
        outs[1][i] = piece[:, PART_B:]

    def cut_y(piece, outs, i):
        outs[0][i] = piece[:half]
        outs[1][i] = piece[half:]

    def cut_x(piece, outs, i):
        outs[0][:, i] = piece[:half]
        outs[1][:, i] = piece[half:]

    col_b, col_c = assemble(place, 1, pieces, [(NZ, n, PART_B), (NZ, n, PART_C)], cut_z)
    along_y = [col_b] + [shift(col_b, "y", by) for by in (1, 2, 3)]
    along_x = [col_c] + [shift(col_c, "x", by) for by in (1, 2, 3)]
    plane_b = assemble(place, 0, along_y, [(NY, half, n, PART_B)] * 2, cut_y)
    plane_c = assemble(place, 2, along_x, [(half, NX, n, PART_C)] * 2, cut_x)
    return both_ways(*plane_b, "x"), both_ways(*plane_c, "y")


def project_kernel(place_ref, n_ref, *refs):
    pieces_b, pieces_c = refs[:8], refs[8:16]
    mine_ref, theirs_ref, wb_ref, wc_ref, sems = refs[16:]
    y, x, me = place_ref[0], place_ref[2], place_ref[3]
    half = NZ // 2
    pairs = []
    for by in range(4):
        for part, lane in enumerate((slice(0, half), slice(half, NZ))):
            pairs.append((pieces_b[2 * by + part], wb_ref.at[:, lane, wrap(x - by, NX)]))
            pairs.append((pieces_c[2 * by + part], wc_ref.at[wrap(y - by, NY), lane]))
    copies = [pltpu.make_async_copy(s, d, sems.at[i]) for i, (s, d) in enumerate(pairs)]
    for copy in copies:
        copy.start()
    for copy in copies:
        copy.wait()
    rows = mine_ref.shape[0]
    n = wb_ref.shape[3]
    parts = ((wb_ref, n_ref[:, :PART_B]), (wc_ref, n_ref[:, PART_B:]))
    wide = half * NX * n
    for row in range(NY):
        for start in (0, half):
            terms = None
            for w_ref, normed in parts:
                w = w_ref[row, start : start + half].reshape(wide, normed.shape[1])
                term = dot(normed, w, ((1,), (1,)))
                terms = term if terms is None else terms + term
            first, second = terms[:rows], terms[rows:]
            at = slice((row * NZ + start) * NX * n, (row * NZ + start) * NX * n + wide)
            mine_ref[:, at] = jnp.where(me == 0, first, second)
            theirs_ref[:, at] = jnp.where(me == 0, second, first)


def project(place, normed, pieces):
    rows = normed.shape[0]
    n = pieces[0].shape[2]
    half = jax.ShapeDtypeStruct((rows // 2, NY * NZ * NX * n), F32)
    hbm = pl.BlockSpec(memory_space=pl.ANY)
    return pl.pallas_call(
        project_kernel,
        in_specs=[pl.BlockSpec(memory_space=pltpu.SMEM), pl.BlockSpec(memory_space=pltpu.VMEM)]
        + [hbm] * len(pieces),
        out_shape=[half, half],
        scratch_shapes=[
            pltpu.VMEM((NY, NZ, NX, n, part), BF) for part in (PART_B, PART_C)
        ]
        + [pltpu.SemaphoreType.DMA((16,))],
        name="project",
    )(place, normed, *pieces)


def whole(queries, keys, values, gain, w_out):
    devices = lax.axis_size(SEQ)
    own = w_out.T
    place = jnp.stack([lax.axis_index(a) for a in SEQ + ("head",)]).astype(jnp.int32)
    parts_b, parts_c = gather(own, place)
    states = local_states(keys, values)
    shares = lax.all_to_all(states, SEQ, 0, 0, tiled=True)
    sums = exclusive_sums(shares.reshape(devices, -1, DH))
    prior = lax.all_to_all(sums.reshape(-1, DH), SEQ, 0, 0, tiled=True)
    normed = attention(queries, keys, values, prior, gain.reshape(1, -1))
    mine, theirs = project(place, normed, parts_b + parts_c)
    other = lax.ppermute(theirs, "head", [(0, 1), (1, 0)])
    return (mine + other).astype(BF)


def solution(mesh):
    torus = jax.sharding.Mesh(mesh.devices.reshape(NY, NZ, NX, 2), SEQ + ("head",))
    return jax.shard_map(
        whole,
        mesh=torus,
        in_specs=(
            P(SEQ, "head"),
            P(SEQ, "head"),
            P(SEQ, "head"),
            P("head"),
            P("head", SEQ),
        ),
        out_specs=P(SEQ + ("head",), None),
        check_vma=False,
    )
```

```python
import jax
import jax.numpy as jnp
from jax import lax
from jax.experimental import pallas as pl
from jax.experimental.pallas import tpu as pltpu
from jax.sharding import PartitionSpec as P


DH = 128
BF = jnp.bfloat16
SMALL = pltpu.CompilerParams(vmem_limit_bytes=16 << 20)
F32 = jnp.float32


def near(*arrays):
    return [pltpu.with_memory_space_constraint(a, pltpu.VMEM) for a in arrays]


def dot(a, b, dims):
    return lax.dot_general(a, b, (dims, ((), ())), preferred_element_type=F32)


def states_kernel(k_ref, v_ref, o_ref):
    for h in range(k_ref.shape[1] // DH):
        c = slice(h * DH, (h + 1) * DH)
        o_ref[c, :] = dot(k_ref[:, c], v_ref[:, c], ((0,), (0,))).astype(BF)


def local_states(keys, values, heads_per_step=4):
    rows, cols = keys.shape
    width = heads_per_step * DH
    spec = pl.BlockSpec((rows, width), lambda i: (0, i))
    return pl.pallas_call(
        states_kernel,
        grid=(cols // width,),
        in_specs=[spec, spec],
        out_specs=pl.BlockSpec((width, DH), lambda i: (i, 0)),
        out_shape=jax.ShapeDtypeStruct((cols, DH), BF),
        compiler_params=SMALL,
        name="local_states",
    )(keys, values)


def running_kernel(x_ref, o_ref):
    def step(j, total):
        o_ref[j] = total.astype(BF)
        return total + x_ref[j].astype(F32)

    lax.fori_loop(0, x_ref.shape[0], step, jnp.zeros(x_ref.shape[1:], F32), unroll=8)


def exclusive_sums(pieces):
    return pl.pallas_call(
        running_kernel,
        out_shape=pltpu.VMEM(pieces.shape, BF),
        compiler_params=SMALL,
        name="exclusive_sums",
    )(*near(pieces))


def attention_kernel(q_ref, k_ref, v_ref, s_ref, g_ref, o_ref):
    rows = q_ref.shape[0]
    t = lax.broadcasted_iota(jnp.int32, (rows, rows), 0)
    s = lax.broadcasted_iota(jnp.int32, (rows, rows), 1)
    causal = t >= s
    for h in range(q_ref.shape[1] // DH):
        c = slice(h * DH, (h + 1) * DH)
        q, k, v = q_ref[:, c], k_ref[:, c], v_ref[:, c]
        scores = jnp.where(causal, dot(q, k, ((1,), (1,))), 0.0)
        high = scores.astype(BF)
        low = (scores - high.astype(F32)).astype(BF)
        attn = dot(q, s_ref[c, :], ((1,), (0,)))
        attn = attn + dot(high, v, ((1,), (0,)))
        attn = attn + dot(low, v, ((1,), (0,)))
        meansq = jnp.mean(attn * attn, axis=-1, keepdims=True)
        o_ref[:, c] = (attn * lax.rsqrt(meansq + 1e-06) * g_ref[:, c]).astype(BF)


def attention(queries, keys, values, prior, gain, heads_per_step=4):
    rows, cols = queries.shape
    width = heads_per_step * DH
    spec = pl.BlockSpec((rows, width), lambda i: (0, i))
    return pl.pallas_call(
        attention_kernel,
        grid=(cols // width,),
        in_specs=[
            spec,
            spec,
            spec,
            pl.BlockSpec((width, DH), lambda i: (i, 0)),
            pl.BlockSpec((1, width), lambda i: (0, i)),
        ],
        out_specs=spec,
        out_shape=jax.ShapeDtypeStruct((rows, cols), BF),
        compiler_params=SMALL,
        name="attention",
    )(queries, keys, values, prior, gain)


SEQ = ("y", "z", "x")
NY, NZ, NX = 4, 8, 4
PART_B, PART_C = 1024, 1024


def shift(block, axis, by):
    pairs = []
    for y in range(NY):
        for z in range(NZ):
            for x in range(NX):
                ty = (y + by) % NY if axis == "y" else y
                tz = (z + by) % NZ if axis == "z" else z
                tx = (x + by) % NX if axis == "x" else x
                pairs.append(((y * NZ + z) * NX + x, (ty * NZ + tz) * NX + tx))
    return lax.ppermute(block, SEQ, pairs)


def wrap(index, count):
    return lax.rem(index + count, count)


def assemble(place, which, pieces, outs, cuts):
    count = len(pieces)

    def kernel(place_ref, *refs):
        for by in range(count):
            cuts(refs[by], refs[count:], wrap(place_ref[which] - by, count))

    vmem = pl.BlockSpec(memory_space=pltpu.VMEM)
    return pl.pallas_call(
        kernel,
        in_specs=[pl.BlockSpec(memory_space=pltpu.SMEM)] + [vmem] * count,
        out_specs=[vmem] * len(outs),
        out_shape=[pltpu.VMEM(o, BF) for o in outs],
        compiler_params=SMALL,
    )(place, *near(*pieces))


def both_ways(low, high, axis):
    below_low = shift(low, axis, 1)
    above_high = shift(high, axis, -1)
    below_high = shift(high, axis, 1)
    above_low = shift(low, axis, -1)
    far_low = shift(below_low, axis, 1)
    far_high = shift(above_high, axis, -1)
    return [low, high, below_low, below_high, far_low, far_high, above_low, above_high]


def gather(own, place):
    n = own.shape[0]
    half = NZ // 2
    pieces = [own] + [shift(own, "z", by) for by in range(1, NZ)]

    def cut_z(piece, outs, i):
        outs[0][i] = piece[:, :PART_B]
        outs[1][i] = piece[:, PART_B:]

    def cut_y(piece, outs, i):
        outs[0][i] = piece[:half]
        outs[1][i] = piece[half:]

    def cut_x(piece, outs, i):
        outs[0][:, i] = piece[:half]
        outs[1][:, i] = piece[half:]

    col_b, col_c = assemble(place, 1, pieces, [(NZ, n, PART_B), (NZ, n, PART_C)], cut_z)
    along_y = [col_b] + [shift(col_b, "y", by) for by in (1, 2, 3)]
    along_x = [col_c] + [shift(col_c, "x", by) for by in (1, 2, 3)]
    plane_b = assemble(place, 0, along_y, [(NY, half, n, PART_B)] * 2, cut_y)
    plane_c = assemble(place, 2, along_x, [(half, NX, n, PART_C)] * 2, cut_x)
    return both_ways(*plane_b, "x"), both_ways(*plane_c, "y")


def multiply(w, normed):
    flat = w.reshape(w.shape[0] * w.shape[1] * w.shape[2], w.shape[3])
    return dot(flat, normed, ((1,), (1,))).reshape(w.shape[:3] + normed.shape[:1])


def split(terms, me):
    rows = terms.shape[-1] // 2
    first, second = terms[..., :rows], terms[..., rows:]
    return jnp.where(me == 0, first, second), jnp.where(me == 0, second, first)


def early_kernel(place_ref, n_ref, *refs):
    pieces, (mine_ref, theirs_ref) = refs[:12], refs[12:]
    y, x, me = place_ref[0], place_ref[2], place_ref[3]
    half = NZ // 2
    lanes = (slice(0, half), slice(half, NZ))
    normed_b, normed_c = n_ref[:, :PART_B], n_ref[:, PART_B:]
    for ref in (mine_ref, theirs_ref):
        ref[:, :, wrap(x - 2, NX)] = jnp.zeros(ref.shape[:2] + ref.shape[3:], F32)
    for i, by in enumerate((0, 1, 3)):
        for part in (0, 1):
            at = (slice(None), lanes[part], wrap(x - by, NX))
            kept, sent = split(multiply(pieces[2 * i + part][...], normed_b), me)
            mine_ref[at] = kept
            theirs_ref[at] = sent
    for i, by in enumerate((0, 1, 3)):
        for part in (0, 1):
            at = (wrap(y - by, NY), lanes[part])
            kept, sent = split(multiply(pieces[6 + 2 * i + part][...], normed_c), me)
            mine_ref[at] += kept
            theirs_ref[at] += sent


def late_kernel(place_ref, n_ref, _mine, _theirs, *refs):
    pieces, (mine_ref, theirs_ref) = refs[:4], refs[4:]
    y, x, me = place_ref[0], place_ref[2], place_ref[3]
    half = NZ // 2
    lanes = (slice(0, half), slice(half, NZ))
    for part in (0, 1):
        for at, piece, normed in (
            ((slice(None), lanes[part], wrap(x - 2, NX)), pieces[part], n_ref[:, :PART_B]),
            ((wrap(y - 2, NY), lanes[part]), pieces[2 + part], n_ref[:, PART_B:]),
        ):
            kept, sent = split(multiply(piece[...], normed), me)
            mine_ref[at] += kept
            theirs_ref[at] += sent


def finish_kernel(mine_ref, other_ref, o_ref):
    wide = o_ref.shape[0]
    for start in range(0, o_ref.shape[1], wide):
        at = slice(start, start + wide)
        o_ref[:, at] = (mine_ref[at] + other_ref[at]).T.astype(BF)


SMEM = pl.BlockSpec(memory_space=pltpu.SMEM)
VMEM = pl.BlockSpec(memory_space=pltpu.VMEM)


def project_early(place, normed, pieces):
    n = pieces[0].shape[2]
    half = pltpu.VMEM((NY, NZ, NX, n, normed.shape[0] // 2), F32)
    return pl.pallas_call(
        early_kernel,
        in_specs=[SMEM] + [VMEM] * 13,
        out_specs=[VMEM, VMEM],
        out_shape=[half, half],
        compiler_params=SMALL,
        name="project_early",
    )(place, *near(normed, *pieces))


def project_late(place, normed, terms, pieces):
    half = pltpu.VMEM(terms[0].shape, F32)
    return pl.pallas_call(
        late_kernel,
        in_specs=[SMEM] + [VMEM] * 7,
        out_specs=[VMEM, VMEM],
        out_shape=[half, half],
        input_output_aliases={2: 0, 3: 1},
        compiler_params=SMALL,
        name="project_late",
    )(place, *near(normed, *terms, *pieces))


def finish(mine, other):
    return pl.pallas_call(
        finish_kernel,
        out_shape=jax.ShapeDtypeStruct((mine.shape[1], mine.shape[0]), BF),
        compiler_params=SMALL,
        name="finish",
    )(*near(mine, other))


def whole(queries, keys, values, gain, w_out):
    devices = lax.axis_size(SEQ)
    own = w_out.T
    place = jnp.stack([lax.axis_index(a) for a in SEQ + ("head",)]).astype(jnp.int32)
    parts_b, parts_c = gather(own, place)
    states = local_states(keys, values)
    shares = lax.all_to_all(states, SEQ, 0, 0, tiled=True)
    sums = exclusive_sums(shares.reshape(devices, -1, DH))
    prior = lax.all_to_all(sums.reshape(-1, DH), SEQ, 0, 0, tiled=True)
    normed = attention(queries, keys, values, prior, gain.reshape(1, -1))
    early = parts_b[:4] + parts_b[6:] + parts_c[:4] + parts_c[6:]
    late = parts_b[4:6] + parts_c[4:6]
    terms = project_early(place, normed, early)
    mine, theirs = project_late(place, normed, terms, late)
    mine, theirs = (a.reshape(-1, a.shape[-1]) for a in (mine, theirs))
    other = lax.ppermute(theirs, "head", [(0, 1), (1, 0)])
    return finish(mine, other)


def solution(mesh):
    torus = jax.sharding.Mesh(mesh.devices.reshape(NY, NZ, NX, 2), SEQ + ("head",))
    return jax.shard_map(
        whole,
        mesh=torus,
        in_specs=(
            P(SEQ, "head"),
            P(SEQ, "head"),
            P(SEQ, "head"),
            P("head"),
            P("head", SEQ),
        ),
        out_specs=P(SEQ + ("head",), None),
        check_vma=False,
    )
```

```python
import jax
import jax.numpy as jnp
from jax import lax
from jax.experimental import pallas as pl
from jax.experimental.pallas import tpu as pltpu
from jax.sharding import PartitionSpec as P


DH = 128
BF = jnp.bfloat16
SMALL = pltpu.CompilerParams(vmem_limit_bytes=16 << 20)
SMEM = pl.BlockSpec(memory_space=pltpu.SMEM)
VMEM = pl.BlockSpec(memory_space=pltpu.VMEM)
F32 = jnp.float32


def near(*arrays):
    return [pltpu.with_memory_space_constraint(a, pltpu.VMEM) for a in arrays]


def away(*arrays):
    return [pltpu.with_memory_space_constraint(a, pltpu.HBM) for a in arrays]


def dot(a, b, dims):
    return lax.dot_general(a, b, (dims, ((), ())), preferred_element_type=F32)


def states_kernel(k_ref, v_ref, o_ref):
    for h in range(k_ref.shape[1] // DH):
        c = slice(h * DH, (h + 1) * DH)
        o_ref[c, :] = dot(k_ref[:, c], v_ref[:, c], ((0,), (0,))).astype(BF)


def local_states(keys, values, heads_per_step=4):
    rows, cols = keys.shape
    width = heads_per_step * DH
    spec = pl.BlockSpec((rows, width), lambda i: (0, i))
    return pl.pallas_call(
        states_kernel,
        grid=(cols // width,),
        in_specs=[spec, spec],
        out_specs=pl.BlockSpec((width, DH), lambda i: (i, 0)),
        out_shape=jax.ShapeDtypeStruct((cols, DH), BF),
        compiler_params=SMALL,
        name="local_states",
    )(*away(keys, values))


def running_kernel(x_ref, o_ref):
    def step(j, total):
        o_ref[j] = total.astype(BF)
        return total + x_ref[j].astype(F32)

    lax.fori_loop(0, x_ref.shape[0], step, jnp.zeros(x_ref.shape[1:], F32), unroll=8)


def exclusive_sums(pieces):
    return pl.pallas_call(
        running_kernel,
        out_shape=pltpu.VMEM(pieces.shape, BF),
        compiler_params=SMALL,
        name="exclusive_sums",
    )(*near(pieces))


def inner_kernel(q_ref, k_ref, v_ref, o_ref):
    rows = q_ref.shape[0]
    t = lax.broadcasted_iota(jnp.int32, (rows, rows), 0)
    s = lax.broadcasted_iota(jnp.int32, (rows, rows), 1)
    causal = t >= s
    for h in range(q_ref.shape[1] // DH):
        c = slice(h * DH, (h + 1) * DH)
        q, k, v = q_ref[:, c], k_ref[:, c], v_ref[:, c]
        scores = jnp.where(causal, dot(q, k, ((1,), (1,))), 0.0)
        high = scores.astype(BF)
        low = (scores - high.astype(F32)).astype(BF)
        o_ref[:, c] = dot(high, v, ((1,), (0,))) + dot(low, v, ((1,), (0,)))


def inner_attention(queries, keys, values, heads_per_step=4):
    rows, cols = queries.shape
    width = heads_per_step * DH
    spec = pl.BlockSpec((rows, width), lambda i: (0, i))
    return pl.pallas_call(
        inner_kernel,
        grid=(cols // width,),
        in_specs=[spec, spec, spec],
        out_specs=spec,
        out_shape=pltpu.VMEM((rows, cols), F32),
        compiler_params=SMALL,
        name="inner_attention",
    )(*away(queries, keys, values))


def normed_kernel(q_ref, i_ref, s_ref, g_ref, o_ref):
    for h in range(q_ref.shape[1] // DH):
        c = slice(h * DH, (h + 1) * DH)
        attn = dot(q_ref[:, c], s_ref[c, :], ((1,), (0,))) + i_ref[:, c]
        meansq = jnp.mean(attn * attn, axis=-1, keepdims=True)
        o_ref[:, c] = (attn * lax.rsqrt(meansq + 1e-06) * g_ref[:, c]).astype(BF)


def normed_attention(queries, inner, prior, gain):
    return pl.pallas_call(
        normed_kernel,
        in_specs=[VMEM] * 4,
        out_specs=VMEM,
        out_shape=pltpu.VMEM(queries.shape, BF),
        compiler_params=SMALL,
        name="normed_attention",
    )(*near(queries, inner, prior, gain))


SEQ = ("y", "z", "x")
NY, NZ, NX = 4, 8, 4
PART_A, PART_B, PART_C = 512, 768, 768
CUT = PART_A + PART_B


def shift(block, axis, by):
    pairs = []
    for y in range(NY):
        for z in range(NZ):
            for x in range(NX):
                ty = (y + by) % NY if axis == "y" else y
                tz = (z + by) % NZ if axis == "z" else z
                tx = (x + by) % NX if axis == "x" else x
                pairs.append(((y * NZ + z) * NX + x, (ty * NZ + tz) * NX + tx))
    return lax.ppermute(block, SEQ, pairs)


def wrap(index, count):
    return lax.rem(index + count, count)


def turn(block, axis, by):
    pairs = []
    for y in range(NY):
        for z in range(NZ):
            for x in range(NX):
                for core in (0, 1):
                    step = -by if core else by
                    ty = (y + step) % NY if axis == "y" else y
                    tz = (z + step) % NZ if axis == "z" else z
                    tx = (x + step) % NX if axis == "x" else x
                    here, there = (y * NZ + z) * NX + x, (ty * NZ + tz) * NX + tx
                    pairs.append((2 * here + core, 2 * there + core))
    return lax.ppermute(block, SEQ + ("head",), pairs)


def around(block, axis):
    first = turn(block, axis, 1)
    second = turn(block, axis, -1)
    return [block, first, second, turn(first, axis, 1)]


def source(place_ref, which, i):
    step = 1 - 2 * place_ref[3]
    return lax.rem(place_ref[which] + 4 - (0, step, -step, 2)[i], 4)


def layer(place_ref, i):
    step = 1 - 2 * place_ref[3]
    return lax.rem(place_ref[1] + NZ - (0, 1, 2, 3, 4, -1, -2, -3)[i] * step, NZ)


def round_z(block):
    ahead, back = [block], [block]
    for step in range(1, 5):
        ahead.append(turn(ahead[-1], "z", 1))
        if step < 4:
            back.append(turn(back[-1], "z", -1))
    return ahead + back[1:]


def assemble(place, sources, pieces, outs, cuts):
    count = len(pieces)

    def kernel(place_ref, *refs):
        for i in range(count):
            cuts(refs[i], refs[count:], sources(place_ref, i))

    vmem = pl.BlockSpec(memory_space=pltpu.VMEM)
    return pl.pallas_call(
        kernel,
        in_specs=[pl.BlockSpec(memory_space=pltpu.SMEM)] + [vmem] * count,
        out_specs=[vmem] * len(outs),
        out_shape=[pltpu.VMEM(o, BF) for o in outs],
        compiler_params=SMALL,
    )(place, *near(*pieces))


def gather_a(own, place):
    n = own.shape[0]

    def cut(piece, outs, i):
        outs[0][i] = piece[...]

    on_x, on_y = (lambda p, i: wrap(p[2] - i, NX)), (lambda p, i: wrap(p[0] - i, NY))
    pieces = [own] + [shift(own, "x", by) for by in (1, 2, 3)]
    (row,) = assemble(place, on_x, pieces, [(NX, n, PART_A)], cut)
    pieces = [row] + [shift(row, "y", by) for by in (1, 2, 3)]
    (plane,) = assemble(place, on_y, pieces, [(NY, NX, n, PART_A)], cut)
    return round_z(plane)


def cut_own_kernel(own_ref, a_ref, copies_ref):
    a_ref[...] = own_ref[:, :PART_A]
    rest = own_ref[:, PART_A:]
    for i in range(NZ):
        copies_ref[i] = rest


def cut_own(own):
    n, depth = own.shape
    return pl.pallas_call(
        cut_own_kernel,
        in_specs=[VMEM],
        out_specs=[VMEM, VMEM],
        out_shape=[pltpu.VMEM((n, PART_A), BF), pltpu.VMEM((NZ, n, depth - PART_A), BF)],
        compiler_params=SMALL,
        name="cut_own",
    )(own)


def cut_column_kernel(column_ref, b_ref, c_ref):
    b_ref[...] = column_ref[:, :, :PART_B]
    c_ref[...] = column_ref[:, :, PART_B:]


def cut_column(column):
    shapes = [column.shape[:2] + (w,) for w in (PART_B, PART_C)]
    return pl.pallas_call(
        cut_column_kernel,
        in_specs=[VMEM],
        out_specs=[VMEM, VMEM],
        out_shape=[pltpu.VMEM(w, BF) for w in shapes],
        compiler_params=SMALL,
        name="cut_column",
    )(*near(column))


def gather_bc(copies, place):
    n = copies.shape[1]

    def cut_y(piece, outs, i):
        outs[0][i] = piece[...]

    def cut_x(piece, outs, i):
        outs[0][:, i] = piece[...]

    column = lax.all_to_all(copies, "z", 0, 0)
    col_b, col_c = cut_column(column)
    on_y, on_x = (lambda p, i: source(p, 0, i)), (lambda p, i: source(p, 2, i))
    along_y, along_x = around(col_b, "y"), around(col_c, "x")
    (plane_b,) = assemble(place, on_y, along_y, [(NY, NZ, n, PART_B)], cut_y)
    (plane_c,) = assemble(place, on_x, along_x, [(NZ, NX, n, PART_C)], cut_x)
    return around(plane_b, "x"), around(plane_c, "y")


def multiply(w, normed):
    flat = w.reshape(w.shape[0] * w.shape[1] * w.shape[2], w.shape[3])
    return dot(flat, normed, ((1,), (1,))).reshape(w.shape[:3] + normed.shape[:1])


def split(terms, me):
    rows = terms.shape[-1] // 2
    first, second = terms[..., :rows], terms[..., rows:]
    return jnp.where(me == 0, first, second), jnp.where(me == 0, second, first)


HALVES = (slice(0, NZ // 2), slice(NZ // 2, NZ))


HALVES = (slice(0, NZ // 2), slice(NZ // 2, NZ))
A_EARLY, A_LATE = (0, 1, 2, 3, 5, 6), (4, 7)


def parts_of(n_ref):
    return n_ref[:, :PART_A], n_ref[:, PART_A:CUT], n_ref[:, CUT:]


def adder(place_ref, mine_ref, theirs_ref):
    def add(at, piece, normed, fresh=False):
        kept, sent = split(multiply(piece, normed), place_ref[3])
        mine_ref[at] = kept if fresh else mine_ref[at] + kept
        theirs_ref[at] = sent if fresh else theirs_ref[at] + sent

    return add


def early_kernel(place_ref, n_ref, *refs):
    count = len(A_EARLY)
    pieces_a, pieces_b, pieces_c = refs[:count], refs[count : count + 3], refs[count + 3 : count + 6]
    mine_ref, theirs_ref = refs[count + 6 :]
    add = adder(place_ref, mine_ref, theirs_ref)
    normed_a, normed_b, normed_c = parts_of(n_ref)
    for ref in (mine_ref, theirs_ref):
        ref[:, :, source(place_ref, 2, 3)] = jnp.zeros(ref.shape[:2] + ref.shape[3:], F32)
    for i in range(3):
        for lane in HALVES:
            at = (slice(None), lane, source(place_ref, 2, i))
            add(at, pieces_b[i][:, lane], normed_b, fresh=True)
    for i in range(3):
        for lane in HALVES:
            add((source(place_ref, 0, i), lane), pieces_c[i][lane], normed_c)
    for i, piece in zip(A_EARLY, pieces_a):
        add((slice(None), layer(place_ref, i)), piece[...], normed_a)


def late_kernel(place_ref, n_ref, _mine, _theirs, *refs):
    count = len(A_LATE)
    pieces_a, (b_ref, c_ref, mine_ref, theirs_ref) = refs[:count], refs[count:]
    add = adder(place_ref, mine_ref, theirs_ref)
    normed_a, normed_b, normed_c = parts_of(n_ref)
    for i, piece in zip(A_LATE, pieces_a):
        add((slice(None), layer(place_ref, i)), piece[...], normed_a)
    for lane in HALVES:
        add((slice(None), lane, source(place_ref, 2, 3)), b_ref[:, lane], normed_b)
        add((source(place_ref, 0, 3), lane), c_ref[lane], normed_c)


def finish_kernel(mine_ref, other_ref, o_ref):
    wide = o_ref.shape[0]
    for start in range(0, o_ref.shape[1], wide):
        at = slice(start, start + wide)
        o_ref[:, at] = (mine_ref[at] + other_ref[at]).T.astype(BF)


def project_early(place, normed, pieces):
    n = pieces[-1].shape[2]
    half = pltpu.VMEM((NY, NZ, NX, n, normed.shape[0] // 2), F32)
    return pl.pallas_call(
        early_kernel,
        in_specs=[SMEM] + [VMEM] * (1 + len(pieces)),
        out_specs=[VMEM, VMEM],
        out_shape=[half, half],
        compiler_params=SMALL,
        name="project_early",
    )(place, *near(normed, *pieces))


def project_late(place, normed, terms, pieces):
    half = pltpu.VMEM(terms[0].shape, F32)
    return pl.pallas_call(
        late_kernel,
        in_specs=[SMEM] + [VMEM] * (3 + len(pieces)),
        out_specs=[VMEM, VMEM],
        out_shape=[half, half],
        input_output_aliases={2: 0, 3: 1},
        compiler_params=SMALL,
        name="project_late",
    )(place, *near(normed, *terms, *pieces))


def finish(mine, other):
    return pl.pallas_call(
        finish_kernel,
        out_shape=jax.ShapeDtypeStruct((mine.shape[1], mine.shape[0]), BF),
        compiler_params=SMALL,
        name="finish",
    )(*near(mine, other))


def whole(queries, keys, values, gain, w_out):
    devices = lax.axis_size(SEQ)
    own = w_out.T
    place = jnp.stack([lax.axis_index(a) for a in SEQ + ("head",)]).astype(jnp.int32)
    first, copies = cut_own(own)
    parts_b, parts_c = gather_bc(copies, place)
    parts_a = gather_a(first, place)
    states = local_states(keys, values)
    shares = lax.all_to_all(states, SEQ, 0, 0, tiled=True)
    sums = exclusive_sums(shares.reshape(devices, -1, DH))
    prior = lax.all_to_all(sums.reshape(-1, DH), SEQ, 0, 0, tiled=True)
    inner = inner_attention(queries, keys, values)
    normed = normed_attention(queries, inner, prior, gain.reshape(1, -1))
    early = [parts_a[i] for i in A_EARLY] + parts_b[:3] + parts_c[:3]
    late = [parts_a[i] for i in A_LATE] + parts_b[3:] + parts_c[3:]
    terms = project_early(place, normed, early)
    mine, theirs = project_late(place, normed, terms, late)
    mine, theirs = (a.reshape(-1, a.shape[-1]) for a in (mine, theirs))
    other = lax.ppermute(theirs, "head", [(0, 1), (1, 0)])
    return finish(mine, other)


def solution(mesh):
    torus = jax.sharding.Mesh(mesh.devices.reshape(NY, NZ, NX, 2), SEQ + ("head",))
    return jax.shard_map(
        whole,
        mesh=torus,
        in_specs=(
            P(SEQ, "head"),
            P(SEQ, "head"),
            P(SEQ, "head"),
            P("head"),
            P("head", SEQ),
        ),
        out_specs=P(SEQ + ("head",), None),
        check_vma=False,
    )
```

```python
import functools

import jax
import jax.numpy as jnp
from jax import lax
from jax.experimental import pallas as pl
from jax.experimental.pallas import tpu as pltpu
from jax.sharding import PartitionSpec as P


DH = 128
BF = jnp.bfloat16
SMALL = pltpu.CompilerParams(vmem_limit_bytes=16 << 20)
SMEM = pl.BlockSpec(memory_space=pltpu.SMEM)
VMEM = pl.BlockSpec(memory_space=pltpu.VMEM)
F32 = jnp.float32


def near(*arrays):
    return [pltpu.with_memory_space_constraint(a, pltpu.VMEM) for a in arrays]


def away(*arrays):
    return [pltpu.with_memory_space_constraint(a, pltpu.HBM) for a in arrays]


def dot(a, b, dims):
    return lax.dot_general(a, b, (dims, ((), ())), preferred_element_type=F32)


def states_kernel(k_ref, v_ref, o_ref):
    for h in range(k_ref.shape[1] // DH):
        c = slice(h * DH, (h + 1) * DH)
        o_ref[c, :] = dot(k_ref[:, c], v_ref[:, c], ((0,), (0,))).astype(BF)


def local_states(keys, values, heads_per_step=4):
    rows, cols = keys.shape
    width = heads_per_step * DH
    spec = pl.BlockSpec((rows, width), lambda i: (0, i))
    return pl.pallas_call(
        states_kernel,
        grid=(cols // width,),
        in_specs=[spec, spec],
        out_specs=pl.BlockSpec((width, DH), lambda i: (i, 0)),
        out_shape=jax.ShapeDtypeStruct((cols, DH), BF),
        compiler_params=SMALL,
        name="local_states",
    )(*away(keys, values))


def running_kernel(x_ref, o_ref):
    def step(j, total):
        o_ref[j] = total.astype(BF)
        return total + x_ref[j].astype(F32)

    lax.fori_loop(0, x_ref.shape[0], step, jnp.zeros(x_ref.shape[1:], F32), unroll=8)


def exclusive_sums(pieces):
    return pl.pallas_call(
        running_kernel,
        out_shape=pltpu.VMEM(pieces.shape, BF),
        compiler_params=SMALL,
        name="exclusive_sums",
    )(*near(pieces))


def inner_kernel(q_ref, k_ref, v_ref, o_ref):
    rows = q_ref.shape[0]
    t = lax.broadcasted_iota(jnp.int32, (rows, rows), 0)
    s = lax.broadcasted_iota(jnp.int32, (rows, rows), 1)
    causal = t >= s
    for h in range(q_ref.shape[1] // DH):
        c = slice(h * DH, (h + 1) * DH)
        q, k, v = q_ref[:, c], k_ref[:, c], v_ref[:, c]
        scores = jnp.where(causal, dot(q, k, ((1,), (1,))), 0.0)
        high = scores.astype(BF)
        low = (scores - high.astype(F32)).astype(BF)
        o_ref[:, c] = dot(high, v, ((1,), (0,))) + dot(low, v, ((1,), (0,)))


def inner_attention(queries, keys, values, heads_per_step=4):
    rows, cols = queries.shape
    width = heads_per_step * DH
    spec = pl.BlockSpec((rows, width), lambda i: (0, i))
    return pl.pallas_call(
        inner_kernel,
        grid=(cols // width,),
        in_specs=[spec, spec, spec],
        out_specs=spec,
        out_shape=pltpu.HBM((rows, cols), F32),
        compiler_params=SMALL,
        name="inner_attention",
    )(*away(queries, keys, values))


def normed_kernel(place_ref, q_ref, i_ref, s_ref, g_ref, o_ref):
    rows = q_ref.shape[0] // 2
    for half in (0, 1):
        at = pl.ds(pl.multiple_of(lax.rem(place_ref[3] + half, 2) * rows, rows), rows)
        t = slice(half * rows, (half + 1) * rows)
        for h in range(q_ref.shape[1] // DH):
            c = slice(h * DH, (h + 1) * DH)
            state = s_ref[pl.ds(pl.multiple_of(pl.program_id(0) * q_ref.shape[1] + h * DH, DH), DH), :]
            attn = dot(q_ref[t, c], state, ((1,), (0,))) + i_ref[t, c]
            meansq = jnp.mean(attn * attn, axis=-1, keepdims=True)
            o_ref[at, c] = (attn * lax.rsqrt(meansq + 1e-06) * g_ref[:, c]).astype(BF)


def normed_attention(place, queries, inner, prior, gain, heads_per_step=4):
    rows, cols = queries.shape
    width = heads_per_step * DH
    spec = pl.BlockSpec((rows, width), lambda i: (0, i))
    return pl.pallas_call(
        normed_kernel,
        grid=(cols // width,),
        in_specs=[SMEM, spec, spec, VMEM, pl.BlockSpec((1, width), lambda i: (0, i))],
        out_specs=spec,
        out_shape=pltpu.VMEM(queries.shape, BF),
        compiler_params=SMALL,
        name="normed_attention",
    )(place, *away(queries, inner), *near(prior), gain)


SEQ = ("y", "z", "x")
NY, NZ, NX = 4, 8, 4
PART_A, PART_B, PART_C = 512, 768, 768
CUT = PART_A + PART_B


def shift(block, axis, by):
    pairs = []
    for y in range(NY):
        for z in range(NZ):
            for x in range(NX):
                ty = (y + by) % NY if axis == "y" else y
                tz = (z + by) % NZ if axis == "z" else z
                tx = (x + by) % NX if axis == "x" else x
                pairs.append(((y * NZ + z) * NX + x, (ty * NZ + tz) * NX + tx))
    return lax.ppermute(block, SEQ, pairs)


def wrap(index, count):
    return lax.rem(index + count, count)


def turn(block, axis, by):
    pairs = []
    for y in range(NY):
        for z in range(NZ):
            for x in range(NX):
                for core in (0, 1):
                    step = -by if core else by
                    ty = (y + step) % NY if axis == "y" else y
                    tz = (z + step) % NZ if axis == "z" else z
                    tx = (x + step) % NX if axis == "x" else x
                    here, there = (y * NZ + z) * NX + x, (ty * NZ + tz) * NX + tx
                    pairs.append((2 * here + core, 2 * there + core))
    return lax.ppermute(block, SEQ + ("head",), pairs)


def around(block, axis):
    first = turn(block, axis, 1)
    second = turn(block, axis, -1)
    return [block, first, second, turn(first, axis, 1)]


def source(place_ref, which, i):
    step = 1 - 2 * place_ref[3]
    return lax.rem(place_ref[which] + 4 - (0, step, -step, 2)[i], 4)


def layer(place_ref, i):
    step = 1 - 2 * place_ref[3]
    return lax.rem(place_ref[1] + NZ - (0, 1, 2, 3, 4, -1, -2, -3)[i] * step, NZ)


def round_z(block):
    ahead, back = [block], [block]
    for step in range(1, 5):
        ahead.append(turn(ahead[-1], "z", 1))
        if step < 4:
            back.append(turn(back[-1], "z", -1))
    return ahead + back[1:]


def assemble(place, sources, pieces, outs, cuts):
    count = len(pieces)

    def kernel(place_ref, *refs):
        for i in range(count):
            cuts(refs[i], refs[count:], sources(place_ref, i))

    vmem = pl.BlockSpec(memory_space=pltpu.VMEM)
    return pl.pallas_call(
        kernel,
        in_specs=[pl.BlockSpec(memory_space=pltpu.SMEM)] + [vmem] * count,
        out_specs=[vmem] * len(outs),
        out_shape=[pltpu.VMEM(o, BF) for o in outs],
        compiler_params=SMALL,
    )(place, *near(*pieces))


def gather_a(own, place):
    n = own.shape[0]

    def cut(piece, outs, i):
        outs[0][i] = piece[...]

    on_x, on_y = (lambda p, i: wrap(p[2] - i, NX)), (lambda p, i: wrap(p[0] - i, NY))
    pieces = [own] + [shift(own, "x", by) for by in (1, 2, 3)]
    (row,) = assemble(place, on_x, pieces, [(NX, n, PART_A)], cut)
    pieces = [row] + [shift(row, "y", by) for by in (1, 2, 3)]
    (plane,) = assemble(place, on_y, pieces, [(NY, NX, n, PART_A)], cut)
    return round_z(plane)


def cut_own_kernel(own_ref, a_ref, copies_ref):
    a_ref[...] = own_ref[:, :PART_A]
    rest = own_ref[:, PART_A:]
    for i in range(NZ):
        copies_ref[i] = rest


def cut_own(own):
    n, depth = own.shape
    return pl.pallas_call(
        cut_own_kernel,
        in_specs=[VMEM],
        out_specs=[VMEM, VMEM],
        out_shape=[pltpu.VMEM((n, PART_A), BF), pltpu.VMEM((NZ, n, depth - PART_A), BF)],
        compiler_params=SMALL,
        name="cut_own",
    )(own)


def cut_column_kernel(column_ref, b_ref, c_ref):
    b_ref[...] = column_ref[:, :, :PART_B]
    c_ref[...] = column_ref[:, :, PART_B:]


def cut_column(column):
    shapes = [column.shape[:2] + (w,) for w in (PART_B, PART_C)]
    return pl.pallas_call(
        cut_column_kernel,
        in_specs=[VMEM],
        out_specs=[VMEM, VMEM],
        out_shape=[pltpu.VMEM(w, BF) for w in shapes],
        compiler_params=SMALL,
        name="cut_column",
    )(*near(column))


def gather_bc(copies, place):
    n = copies.shape[1]

    def cut_y(piece, outs, i):
        outs[0][i] = piece[...]

    def cut_x(piece, outs, i):
        outs[0][:, i] = piece[...]

    column = lax.all_to_all(copies, "z", 0, 0)
    col_b, col_c = cut_column(column)
    on_y, on_x = (lambda p, i: source(p, 0, i)), (lambda p, i: source(p, 2, i))
    along_y, along_x = around(col_b, "y"), around(col_c, "x")
    (plane_b,) = assemble(place, on_y, along_y, [(NY, NZ, n, PART_B)], cut_y)
    (plane_c,) = assemble(place, on_x, along_x, [(NZ, NX, n, PART_C)], cut_x)
    return around(plane_b, "x"), around(plane_c, "y")


def multiply(w, normed):
    flat = w.reshape(w.shape[0] * w.shape[1] * w.shape[2], w.shape[3])
    return dot(flat, normed, ((1,), (1,))).reshape(w.shape[:3] + normed.shape[:1])


HALVES = (slice(0, NZ // 2), slice(NZ // 2, NZ))
STAGES = (((0, 1, 2, 5, 6), (0, 1)), ((3, 7), (2,)), ((4,), (3,)))


def project_kernel(stage, place_ref, n_ref, *refs):
    from_a, from_bc = STAGES[stage]
    fresh = stage == 0
    refs = refs if fresh else refs[2:]
    a_refs, refs = refs[: len(from_a)], refs[len(from_a) :]
    b_refs, refs = refs[: len(from_bc)], refs[len(from_bc) :]
    c_refs, (mine_ref, theirs_ref) = refs[: len(from_bc)], refs[len(from_bc) :]
    rows = mine_ref.shape[-1]
    normed_a, normed_b, normed_c = n_ref[:, :PART_A], n_ref[:, PART_A:CUT], n_ref[:, CUT:]

    def add(at, piece, normed, fresh=False):
        terms = multiply(piece, normed)
        kept, sent = terms[..., :rows], terms[..., rows:]
        mine_ref[at] = kept if fresh else mine_ref[at] + kept
        theirs_ref[at] = sent if fresh else theirs_ref[at] + sent

    if fresh:
        for i in (2, 3):
            for ref in (mine_ref, theirs_ref):
                ref[:, :, source(place_ref, 2, i)] = jnp.zeros(ref.shape[:2] + ref.shape[3:], F32)
    for i, piece in zip(from_bc, b_refs):
        for lane in HALVES:
            add((slice(None), lane, source(place_ref, 2, i)), piece[:, lane], normed_b, fresh)
    for i, piece in zip(from_bc, c_refs):
        for lane in HALVES:
            add((source(place_ref, 0, i), lane), piece[lane], normed_c)
    for i, piece in zip(from_a, a_refs):
        add((slice(None), layer(place_ref, i)), piece[...], normed_a)


def finish_kernel(mine_ref, other_ref, o_ref):
    wide = o_ref.shape[0]
    for start in range(0, o_ref.shape[1], wide):
        at = slice(start, start + wide)
        o_ref[:, at] = (mine_ref[at] + other_ref[at]).T.astype(BF)


def project(stage, place, normed, terms, parts_a, parts_b, parts_c):
    from_a, from_bc = STAGES[stage]
    pieces = [parts_a[i] for i in from_a] + [p[i] for p in (parts_b, parts_c) for i in from_bc]
    half = pltpu.VMEM((NY, NZ, NX, pieces[0].shape[2], normed.shape[0] // 2), F32)
    return pl.pallas_call(
        functools.partial(project_kernel, stage),
        in_specs=[SMEM] + [VMEM] * (1 + len(terms) + len(pieces)),
        out_specs=[VMEM, VMEM],
        out_shape=[half, half],
        input_output_aliases={2: 0, 3: 1} if terms else {},
        compiler_params=SMALL,
    )(place, *near(normed, *terms, *pieces))


def finish(mine, other):
    return pl.pallas_call(
        finish_kernel,
        out_shape=jax.ShapeDtypeStruct((mine.shape[1], mine.shape[0]), BF),
        compiler_params=SMALL,
        name="finish",
    )(*near(mine, other))


def whole(queries, keys, values, gain, w_out):
    devices = lax.axis_size(SEQ)
    own = w_out.T
    place = jnp.stack([lax.axis_index(a) for a in SEQ + ("head",)]).astype(jnp.int32)
    first, copies = cut_own(own)
    parts_b, parts_c = gather_bc(copies, place)
    parts_a = gather_a(first, place)
    states = local_states(keys, values)
    shares = lax.all_to_all(states, SEQ, 0, 0, tiled=True)
    sums = exclusive_sums(shares.reshape(devices, -1, DH))
    prior = lax.all_to_all(sums.reshape(-1, DH), SEQ, 0, 0, tiled=True)
    inner = inner_attention(queries, keys, values)
    normed = normed_attention(place, queries, inner, prior, gain.reshape(1, -1))
    terms = ()
    for stage in range(len(STAGES)):
        terms = project(stage, place, normed, terms, parts_a, parts_b, parts_c)
    mine, theirs = (a.reshape(-1, a.shape[-1]) for a in terms)
    other = lax.ppermute(theirs, "head", [(0, 1), (1, 0)])
    return finish(mine, other)


def solution(mesh):
    torus = jax.sharding.Mesh(mesh.devices.reshape(NY, NZ, NX, 2), SEQ + ("head",))
    return jax.shard_map(
        whole,
        mesh=torus,
        in_specs=(
            P(SEQ, "head"),
            P(SEQ, "head"),
            P(SEQ, "head"),
            P("head"),
            P("head", SEQ),
        ),
        out_specs=P(SEQ + ("head",), None),
        check_vma=False,
    )
```

```python
import functools

import jax
import jax.numpy as jnp
from jax import lax
from jax.experimental import pallas as pl
from jax.experimental.pallas import tpu as pltpu
from jax.sharding import PartitionSpec as P


DH = 128
BF = jnp.bfloat16
SMALL = pltpu.CompilerParams(vmem_limit_bytes=16 << 20)
SMEM = pl.BlockSpec(memory_space=pltpu.SMEM)
VMEM = pl.BlockSpec(memory_space=pltpu.VMEM)
F32 = jnp.float32


def near(*arrays):
    return [pltpu.with_memory_space_constraint(a, pltpu.VMEM) for a in arrays]


def away(*arrays):
    return [pltpu.with_memory_space_constraint(a, pltpu.HBM) for a in arrays]


def dot(a, b, dims):
    return lax.dot_general(a, b, (dims, ((), ())), preferred_element_type=F32)


def states_kernel(k_ref, v_ref, o_ref):
    for h in range(k_ref.shape[1] // DH):
        c = slice(h * DH, (h + 1) * DH)
        o_ref[c, :] = dot(k_ref[:, c], v_ref[:, c], ((0,), (0,))).astype(BF)


def local_states(keys, values, heads_per_step=4):
    rows, cols = keys.shape
    width = heads_per_step * DH
    spec = pl.BlockSpec((rows, width), lambda i: (0, i))
    return pl.pallas_call(
        states_kernel,
        grid=(cols // width,),
        in_specs=[spec, spec],
        out_specs=pl.BlockSpec((width, DH), lambda i: (i, 0)),
        out_shape=jax.ShapeDtypeStruct((cols, DH), BF),
        compiler_params=SMALL,
        name="local_states",
    )(*away(keys, values))


def running_kernel(x_ref, o_ref):
    def step(j, total):
        o_ref[j] = total.astype(BF)
        return total + x_ref[j].astype(F32)

    lax.fori_loop(0, x_ref.shape[0], step, jnp.zeros(x_ref.shape[1:], F32), unroll=8)


def exclusive_sums(pieces):
    return pl.pallas_call(
        running_kernel,
        out_shape=pltpu.VMEM(pieces.shape, BF),
        compiler_params=SMALL,
        name="exclusive_sums",
    )(*near(pieces))


def inner_kernel(q_ref, k_ref, v_ref, o_ref):
    rows = q_ref.shape[0]
    t = lax.broadcasted_iota(jnp.int32, (rows, rows), 0)
    s = lax.broadcasted_iota(jnp.int32, (rows, rows), 1)
    causal = t >= s
    for h in range(q_ref.shape[1] // DH):
        c = slice(h * DH, (h + 1) * DH)
        q, k, v = q_ref[:, c], k_ref[:, c], v_ref[:, c]
        scores = jnp.where(causal, dot(q, k, ((1,), (1,))), 0.0)
        high = scores.astype(BF)
        low = (scores - high.astype(F32)).astype(BF)
        o_ref[:, c] = dot(high, v, ((1,), (0,))) + dot(low, v, ((1,), (0,)))


def inner_attention(queries, keys, values, heads_per_step=4):
    rows, cols = queries.shape
    width = heads_per_step * DH
    spec = pl.BlockSpec((rows, width), lambda i: (0, i))
    return pl.pallas_call(
        inner_kernel,
        grid=(cols // width,),
        in_specs=[spec, spec, spec],
        out_specs=spec,
        out_shape=pltpu.HBM((rows, cols), F32),
        compiler_params=SMALL,
        name="inner_attention",
    )(*away(queries, keys, values))


def normed_kernel(place_ref, q_ref, i_ref, s_ref, g_ref, o_ref):
    rows = q_ref.shape[0] // 2
    for half in (0, 1):
        at = pl.ds(pl.multiple_of(lax.rem(place_ref[3] + half, 2) * rows, rows), rows)
        t = slice(half * rows, (half + 1) * rows)
        for h in range(q_ref.shape[1] // DH):
            c = slice(h * DH, (h + 1) * DH)
            state = s_ref[pl.ds(pl.multiple_of(pl.program_id(0) * q_ref.shape[1] + h * DH, DH), DH), :]
            attn = dot(q_ref[t, c], state, ((1,), (0,))) + i_ref[t, c]
            meansq = jnp.mean(attn * attn, axis=-1, keepdims=True)
            o_ref[at, c] = (attn * lax.rsqrt(meansq + 1e-06) * g_ref[:, c]).astype(BF)


def normed_attention(place, queries, inner, prior, gain, heads_per_step=4):
    rows, cols = queries.shape
    width = heads_per_step * DH
    spec = pl.BlockSpec((rows, width), lambda i: (0, i))
    return pl.pallas_call(
        normed_kernel,
        grid=(cols // width,),
        in_specs=[SMEM, spec, spec, VMEM, pl.BlockSpec((1, width), lambda i: (0, i))],
        out_specs=spec,
        out_shape=pltpu.VMEM(queries.shape, BF),
        compiler_params=SMALL,
        name="normed_attention",
    )(place, *away(queries, inner), *near(prior), gain)


SEQ = ("y", "z", "x")
NY, NZ, NX = 4, 8, 4
PART_A, PART_B, PART_C = 512, 768, 768
CUT = PART_A + PART_B


def shift(block, axis, by):
    pairs = []
    for y in range(NY):
        for z in range(NZ):
            for x in range(NX):
                ty = (y + by) % NY if axis == "y" else y
                tz = (z + by) % NZ if axis == "z" else z
                tx = (x + by) % NX if axis == "x" else x
                pairs.append(((y * NZ + z) * NX + x, (ty * NZ + tz) * NX + tx))
    return lax.ppermute(block, SEQ, pairs)


def wrap(index, count):
    return lax.rem(index + count, count)


def turn(block, axis, by):
    pairs = []
    for y in range(NY):
        for z in range(NZ):
            for x in range(NX):
                for core in (0, 1):
                    step = -by if core else by
                    ty = (y + step) % NY if axis == "y" else y
                    tz = (z + step) % NZ if axis == "z" else z
                    tx = (x + step) % NX if axis == "x" else x
                    here, there = (y * NZ + z) * NX + x, (ty * NZ + tz) * NX + tx
                    pairs.append((2 * here + core, 2 * there + core))
    return lax.ppermute(block, SEQ + ("head",), pairs)


def around(block, axis):
    first = turn(block, axis, 1)
    second = turn(block, axis, -1)
    return [block, first, second, turn(first, axis, 1)]


def source(place_ref, which, i):
    step = 1 - 2 * place_ref[3]
    return lax.rem(place_ref[which] + 4 - (0, step, -step, 2)[i], 4)


def layer(place_ref, i):
    step = 1 - 2 * place_ref[3]
    return lax.rem(place_ref[1] + NZ - (0, 1, 2, 3, 4, -1, -2, -3)[i] * step, NZ)


def round_z(block):
    ahead, back = [block], [block]
    for _ in range(1, 4):
        ahead.append(turn(ahead[-1], "z", 1))
        back.append(turn(back[-1], "z", -1))
    return ahead + [turn(block, "z", 4)] + back[1:]


def assemble(place, sources, pieces, outs, cuts, stored=0):
    count = len(pieces)

    def kernel(place_ref, *refs):
        for i in range(count):
            cuts(refs[i], refs[count:], sources(place_ref, i))

    vmem = pl.BlockSpec(memory_space=pltpu.VMEM)
    return pl.pallas_call(
        kernel,
        in_specs=[pl.BlockSpec(memory_space=pltpu.SMEM)] + [vmem] * count,
        out_specs=[vmem] * len(outs),
        out_shape=[pltpu.VMEM(o, BF) for o in outs],
        compiler_params=SMALL,
    )(place, *away(*pieces[:stored]), *near(*pieces[stored:]))


def gather_a(own, place):
    n = own.shape[0]

    def cut(piece, outs, i):
        outs[0][i] = piece[...]

    on_x, on_y = (lambda p, i: wrap(p[2] - i, NX)), (lambda p, i: wrap(p[0] - i, NY))
    pieces = [own] + [shift(own, "x", by) for by in (1, 2, 3)]
    (row,) = assemble(place, on_x, pieces, [(NX, n, PART_A)], cut)
    pieces = [row] + [shift(row, "y", by) for by in (1, 2, 3)]
    (plane,) = assemble(place, on_y, pieces, [(NY, NX, n, PART_A)], cut)
    return round_z(plane)


def cut_own_kernel(own_ref, a_ref, copies_ref):
    a_ref[...] = own_ref[:, :PART_A]
    rest = own_ref[:, PART_A:]
    for i in range(NZ):
        copies_ref[i] = rest


def cut_own(own):
    n, depth = own.shape
    return pl.pallas_call(
        cut_own_kernel,
        in_specs=[VMEM],
        out_specs=[VMEM, VMEM],
        out_shape=[pltpu.VMEM((n, PART_A), BF), pltpu.VMEM((NZ, n, depth - PART_A), BF)],
        compiler_params=SMALL,
        name="cut_own",
    )(own)


def cut_column_kernel(column_ref, b_ref, c_ref):
    b_ref[...] = column_ref[:, :, :PART_B]
    c_ref[...] = column_ref[:, :, PART_B:]


def cut_column(column):
    shapes = [column.shape[:2] + (w,) for w in (PART_B, PART_C)]
    return pl.pallas_call(
        cut_column_kernel,
        in_specs=[VMEM],
        out_specs=[VMEM, VMEM],
        out_shape=[pltpu.VMEM(w, BF) for w in shapes],
        compiler_params=SMALL,
        name="cut_column",
    )(*near(column))


def gather_bc(copies, place):
    n = copies.shape[1]

    def cut_y(piece, outs, i):
        outs[0][i] = piece[...]

    def cut_x(piece, outs, i):
        outs[0][:, i] = piece[...]

    column = lax.all_to_all(copies, "z", 0, 0)
    col_b, col_c = cut_column(column)
    on_y, on_x = (lambda p, i: source(p, 0, i)), (lambda p, i: source(p, 2, i))
    along_y, along_x = around(col_b, "y"), around(col_c, "x")
    (plane_b,) = assemble(place, on_y, along_y, [(NY, NZ, n, PART_B)], cut_y)
    (plane_c,) = assemble(place, on_x, along_x, [(NZ, NX, n, PART_C)], cut_x, 2)
    return around(plane_b, "x"), around(plane_c, "y")


def multiply(w, normed):
    flat = w.reshape(w.shape[0] * w.shape[1] * w.shape[2], w.shape[3])
    return dot(flat, normed, ((1,), (1,))).reshape(w.shape[:3] + normed.shape[:1])


HALVES = (slice(0, NZ // 2), slice(NZ // 2, NZ))
STAGES = (((0, 1, 5), (0, 1)), ((2, 4, 6), (2,)), ((3, 7), (3,)))


def project_kernel(stage, place_ref, n_ref, *refs):
    from_a, from_bc = STAGES[stage]
    fresh = stage == 0
    refs = refs if fresh else refs[2:]
    a_refs, refs = refs[: len(from_a)], refs[len(from_a) :]
    b_refs, refs = refs[: len(from_bc)], refs[len(from_bc) :]
    c_refs, (mine_ref, theirs_ref) = refs[: len(from_bc)], refs[len(from_bc) :]
    rows = mine_ref.shape[-1]
    normed_a, normed_b, normed_c = n_ref[:, :PART_A], n_ref[:, PART_A:CUT], n_ref[:, CUT:]

    def add(at, piece, normed, fresh=False):
        terms = multiply(piece, normed)
        kept, sent = terms[..., :rows], terms[..., rows:]
        mine_ref[at] = kept if fresh else mine_ref[at] + kept
        theirs_ref[at] = sent if fresh else theirs_ref[at] + sent

    if fresh:
        for i in (2, 3):
            for ref in (mine_ref, theirs_ref):
                ref[:, :, source(place_ref, 2, i)] = jnp.zeros(ref.shape[:2] + ref.shape[3:], F32)
    for i, piece in zip(from_bc, b_refs):
        for lane in HALVES:
            add((slice(None), lane, source(place_ref, 2, i)), piece[:, lane], normed_b, fresh)
    for i, piece in zip(from_bc, c_refs):
        for lane in HALVES:
            add((source(place_ref, 0, i), lane), piece[lane], normed_c)
    for i, piece in zip(from_a, a_refs):
        add((slice(None), layer(place_ref, i)), piece[...], normed_a)


def finish_kernel(mine_ref, other_ref, o_ref):
    wide = o_ref.shape[0]
    for start in range(0, o_ref.shape[1], wide):
        at = slice(start, start + wide)
        o_ref[:, at] = (mine_ref[at] + other_ref[at]).T.astype(BF)


def project(stage, place, normed, terms, parts_a, parts_b, parts_c):
    from_a, from_bc = STAGES[stage]
    pieces = [parts_a[i] for i in from_a] + [p[i] for p in (parts_b, parts_c) for i in from_bc]
    half = pltpu.VMEM((NY, NZ, NX, pieces[0].shape[2], normed.shape[0] // 2), F32)
    return pl.pallas_call(
        functools.partial(project_kernel, stage),
        in_specs=[SMEM] + [VMEM] * (1 + len(terms) + len(pieces)),
        out_specs=[VMEM, VMEM],
        out_shape=[half, half],
        input_output_aliases={2: 0, 3: 1} if terms else {},
        compiler_params=SMALL,
    )(place, *near(normed, *terms, *pieces))


def finish(mine, other):
    return pl.pallas_call(
        finish_kernel,
        out_shape=jax.ShapeDtypeStruct((mine.shape[1], mine.shape[0]), BF),
        compiler_params=SMALL,
        name="finish",
    )(*near(mine, other))


def whole(queries, keys, values, gain, w_out):
    devices = lax.axis_size(SEQ)
    own = w_out.T
    place = jnp.stack([lax.axis_index(a) for a in SEQ + ("head",)]).astype(jnp.int32)
    first, copies = cut_own(own)
    parts_b, parts_c = gather_bc(copies, place)
    parts_a = gather_a(first, place)
    states = local_states(keys, values)
    shares = lax.all_to_all(states, SEQ, 0, 0, tiled=True)
    sums = exclusive_sums(shares.reshape(devices, -1, DH))
    prior = lax.all_to_all(sums.reshape(-1, DH), SEQ, 0, 0, tiled=True)
    inner = inner_attention(queries, keys, values)
    normed = normed_attention(place, queries, inner, prior, gain.reshape(1, -1))
    terms = ()
    for stage in range(len(STAGES)):
        terms = project(stage, place, normed, terms, parts_a, parts_b, parts_c)
    mine, theirs = (a.reshape(-1, a.shape[-1]) for a in terms)
    other = lax.ppermute(theirs, "head", [(0, 1), (1, 0)])
    return finish(mine, other)


def solution(mesh):
    torus = jax.sharding.Mesh(mesh.devices.reshape(NY, NZ, NX, 2), SEQ + ("head",))
    return jax.shard_map(
        whole,
        mesh=torus,
        in_specs=(
            P(SEQ, "head"),
            P(SEQ, "head"),
            P(SEQ, "head"),
            P("head"),
            P("head", SEQ),
        ),
        out_specs=P(SEQ + ("head",), None),
        check_vma=False,
    )
```
